32 devices in a mesh: grp: 2 (over x), ta: 4 (over y, core), gz: 4 (over z).
Axes of the slice: x: 2, y: 2, z: 4, core: 2. Of those that a mesh axis runs over, the one named last changes fastest.
Arguments:
- coarse_links: bfloat16 [4, 4, 16, 9, 128, 128], P('ta', 'gz'), may hold values from -5 to 5
- right_sides: float32 [16, 4, 4, 16, 128], P(None, 'ta', 'gz', 'grp'), may hold values from -12 to 12
Outputs:
- solution: float32 [16, 4, 4, 16, 128], P(None, 'ta', 'gz', 'grp')
- residual: float32 [16, 4, 4, 16, 128], P(None, 'ta', 'gz', 'grp')
The draws below stay inside these ranges and needn't reach their ends.
All inputs are finite; a program needn't handle non-finite values.
Results may differ from the reference program's by a relative error of at most 0.015.
The reference program's roundings to bfloat16 on the way (of `direction`) count: a program that leaves them out, or rounds other values in their place, can miss the bound.
Values may be sent and summed in bfloat16 or wider, within the bound.
No kernel may reach another device: no remote copies, remote signals or barrier semaphores. Data moves between devices by JAX's collectives and lax.ppermute only.
A program may use at most 64 MiB of HBM per device.

```python
import math
import jax
import jax.numpy as jnp
import numpy as np
from jax import lax

C = 128
LX = 4
LY = 4
ITERS = 4
XY = 16
LT = 4
LZ = 4
RHS = 16


def draw_coarse_links(key, part):
    extent = (LT, LZ, XY, 9, C, C)
    entry_key, factor_key = jax.random.split(key)
    entries = jnp.clip(jax.random.normal(entry_key, extent, jnp.float32), -4.0, 4.0)
    factor = jax.random.uniform(factor_key, extent[:4] + (1, 1), jnp.float32, 0.5, 1.5)
    row_ids = lax.broadcasted_iota(jnp.int32, extent, 4)
    col_ids = lax.broadcasted_iota(jnp.int32, extent, 5)
    direction = lax.broadcasted_iota(jnp.int32, extent, 3)
    centre = (direction == 0).astype(jnp.float32)
    identity = (row_ids == col_ids).astype(jnp.float32)
    spread = (0.3 + 0.2 * centre) / math.sqrt(C)
    values = entries * factor * spread + 4.0 * centre * identity
    return values.astype(jnp.bfloat16)


def draw_right_sides(key, part):
    extent = (RHS, LT, LZ, XY, C)
    slices = lax.broadcasted_iota(jnp.int32, extent, 1).astype(jnp.float32)
    spread = 1.0 + 2.0 * slices / max(LT - 1, 1)
    values = jnp.clip(jax.random.normal(key, extent, jnp.float32), -4.0, 4.0) * spread
    return values


def setup_inputs(seed: int = 0) -> dict:
    splits = jax.random.split(jax.random.key(seed), 3)
    return {
        "coarse_links": draw_coarse_links(jax.random.fold_in(splits[2], 71), 0),
        "right_sides": draw_right_sides(jax.random.fold_in(splits[2], 71), 0),
    }


def site_table():
    site_ids = np.arange(LX * LY)
    column = site_ids % LX
    row_of = site_ids // LX
    forward_x = row_of * LX + (column + 1) % LX
    backward_x = row_of * LX + (column - 1) % LX
    forward_y = (row_of + 1) % LY * LX + column
    backward_y = (row_of - 1) % LY * LX + column
    return np.stack([forward_x, backward_x, forward_y, backward_y], axis=1).astype(np.int32)

def apply_slab(slab_links, centre, after_t, before_t, table):
    extent = centre.shape
    planar = jnp.take(centre, jnp.asarray(table.reshape(-1)), axis=2).reshape(extent[0], extent[1], extent[2], 4, extent[3])
    upper_z = jnp.roll(centre, -1, axis=1)
    lower_z = jnp.roll(centre, 1, axis=1)
    stacked = jnp.concatenate([centre[:, :, :, None, :], planar, upper_z[:, :, :, None, :], lower_z[:, :, :, None, :], after_t[:, :, :, None, :], before_t[:, :, :, None, :]], axis=3)
    return jnp.einsum('zsmab,rzsmb->rzsa', slab_links.astype(jnp.float32), stacked.astype(jnp.float32), precision=lax.Precision.HIGHEST)

def apply_operator(coarse_links, field):
    table = site_table()

    def slab(slab_index):
        centre = jnp.take(field, slab_index, axis=1)
        after_t = jnp.take(field, (slab_index + 1) % LT, axis=1)
        before_t = jnp.take(field, (slab_index + LT - 1) % LT, axis=1)
        return apply_slab(coarse_links[slab_index], centre, after_t, before_t, table)
    result = lax.map(slab, jnp.arange(LT, dtype=jnp.int32))
    return jnp.transpose(result, (1, 0, 2, 3, 4))

def inner(left, right):
    return lax.optimization_barrier(jnp.sum(left * right, axis=(1, 2, 3, 4)))

def expand(values):
    return values.reshape(-1, 1, 1, 1, 1)

def reference(coarse_links, right_sides):
    solution = jnp.zeros_like(right_sides)
    residual = right_sides
    basis_q = []
    basis_p = []
    for iteration in range(ITERS):
        direction = residual.astype(jnp.bfloat16)
        mapped = apply_operator(coarse_links, direction)
        search = direction.astype(jnp.float32)
        coefficients = [inner(older, mapped) for older in basis_q]
        ortho_q = mapped
        ortho_p = search
        for older_q, older_p, weight in zip(basis_q, basis_p, coefficients):
            ortho_q = ortho_q - expand(weight) * older_q
            ortho_p = ortho_p - expand(weight) * older_p
        squared = inner(ortho_q, ortho_q)
        projected = inner(ortho_q, residual)
        inverse = 1.0 / jnp.sqrt(squared)
        new_q = ortho_q * expand(inverse)
        new_p = ortho_p * expand(inverse)
        alpha = projected * inverse
        solution = solution + expand(alpha) * new_p
        residual = residual - expand(alpha) * new_q
        basis_q.append(new_q)
        basis_p.append(new_p)
    return (solution, residual)
```

```python
import functools

import jax
import jax.numpy as jnp
import numpy as np
from jax import lax
from jax.experimental import pallas as pl
from jax.experimental.pallas import tpu as pltpu
from jax.sharding import PartitionSpec as P

LX = 4
LY = 4
ITERS = 4
AXES = ("grp", "ta", "gz")
LANES = 128


def site_table():
    site_ids = np.arange(LX * LY)
    column = site_ids % LX
    row_of = site_ids // LX
    forward_x = row_of * LX + (column + 1) % LX
    backward_x = row_of * LX + (column - 1) % LX
    forward_y = (row_of + 1) % LY * LX + column
    backward_y = (row_of - 1) % LY * LX + column
    return np.stack([forward_x, backward_x, forward_y, backward_y], axis=1).astype(np.int32)


def pairings(count):
    if count % 2 == 0:
        first = [(i, i ^ 1) for i in range(count)]
        second = [(i, (i + 1) % count if i % 2 else (i - 1) % count) for i in range(count)]
        return first, second, True
    up = [((i + 1) % count, i) for i in range(count)]
    return up, [(target, source) for source, target in up], False


def exchange(block):
    count = lax.axis_size("grp")
    blocks = []
    for shift in range(1, count):
        blocks.append(lax.ppermute(block, "grp", [((i + shift) % count, i) for i in range(count)]))
    for axis in ("ta", "gz"):
        first, second, _ = pairings(lax.axis_size(axis))
        blocks += [lax.ppermute(block, axis, first), lax.ppermute(block, axis, second)]
    return blocks


def arranged_links(coarse_links, site_count):
    offset = lax.axis_index("grp") * site_count
    part = lax.dynamic_slice_in_dim(coarse_links[0, 0], offset, site_count, 0)
    pieces = [part[:, :5]]
    for axis, base in (("ta", 7), ("gz", 5)):
        if pairings(lax.axis_size(axis))[2]:
            odd = lax.axis_index(axis) % 2
            pieces.append(lax.dynamic_slice_in_dim(part, base + odd, 1, 1))
            pieces.append(lax.dynamic_slice_in_dim(part, base + 1 - odd, 1, 1))
        else:
            pieces.append(part[:, base : base + 2])
    ordered = jnp.concatenate(pieces, axis=1)
    return jnp.swapaxes(ordered, 2, 3).reshape(site_count, -1, ordered.shape[2])


def columns(gathered, count, rhs):
    total = jnp.sum(gathered, axis=0, keepdims=True)
    spread = jnp.broadcast_to(total, (rhs, total.shape[1]))
    lane = lax.broadcasted_iota(jnp.int32, spread.shape, 1)
    row = lax.broadcasted_iota(jnp.int32, spread.shape, 0)
    return [
        jnp.sum(jnp.where(lane == row + index * rhs, spread, 0.0), axis=1, keepdims=True)
        for index in range(count)
    ]


def weights(gathered, previous, rhs):
    values = columns(gathered, previous + 2, rhs)
    coefficients = values[:previous]
    squared, projected = values[previous], values[previous + 1]
    for value in coefficients:
        squared = squared - value * value
    inverse = 1.0 / jnp.sqrt(squared)
    return coefficients, inverse, projected * inverse


def products(rows, links_ref, table_ref, plane_ref, blocks):
    plane = [value for block in blocks[: rows["plane"]] for value in block]
    neighbours = rows["neighbours"]
    if neighbours is None:
        for index, value in enumerate(plane):
            plane_ref[index] = value
    result = []
    for site in range(rows["sites"]):
        parts = [blocks[0][site]]
        if neighbours is None:
            parts += [plane_ref[table_ref[site, hop]] for hop in range(4)]
        else:
            parts += [plane[index] for index in neighbours[site]]
        parts += [block[site] for block in blocks[rows["plane"] :]]
        result.append(
            jnp.dot(
                jnp.concatenate(parts, axis=1),
                links_ref[site],
                preferred_element_type=jnp.float32,
            )
        )
    return result


def inner_rows(pairs, out_ref):
    stacked = []
    for left, right in pairs:
        total = left[0] * right[0]
        for a, b in zip(left[1:], right[1:]):
            total = total + a * b
        stacked.append(total)
    height = sum(value.shape[0] for value in stacked)
    if out_ref.shape[1] > height:
        stacked.append(jnp.zeros((out_ref.shape[1] - height, stacked[0].shape[1]), jnp.float32))
    table = jnp.concatenate(stacked, axis=0)
    ones = jnp.ones((out_ref.shape[0], table.shape[1]), jnp.float32)
    out_ref[...] = lax.dot_general(
        ones,
        table,
        (((1,), (1,)), ((), ())),
        precision=lax.Precision.HIGHEST,
        preferred_element_type=jnp.float32,
    )


def first_kernel(rows, table_ref, links_ref, *refs):
    count = rows["blocks"]
    residual_refs, (mapped_ref, dots_ref, plane_ref) = refs[:count], refs[count:]
    sites = range(rows["sites"])
    blocks = [[ref[site].astype(jnp.bfloat16) for site in sites] for ref in residual_refs]
    mapped = products(rows, links_ref, table_ref, plane_ref, blocks)
    own = [residual_refs[0][site] for site in sites]
    for site in sites:
        mapped_ref[site] = mapped[site]
    inner_rows([(mapped, mapped), (mapped, own)], dots_ref)


def next_kernel(rows, previous, table_ref, links_ref, gathered_ref, *refs):
    count = rows["blocks"]
    sites = range(rows["sites"])
    refs = list(refs)
    mapped_in, refs = refs[:count], refs[count:]
    if previous == 0:
        residual_in, refs = refs[:count], refs[count:]
    else:
        residual_in, refs = [refs[0].at[index] for index in range(count)], refs[1:]
    basis, refs = refs[:previous], refs[previous:]
    mapped_ref, dots_ref, residual_ref, new_ref, plane_ref = refs
    rhs = mapped_in[0].shape[1]
    coefficients, inverse, alpha = weights(gathered_ref[...], previous, rhs)
    blocks = []
    own = []
    for index in range(count):
        block = []
        for site in sites:
            q = mapped_in[index][site]
            for weight, older in zip(coefficients, basis):
                q = q - weight * older[index, site]
            q = q * inverse
            new_ref[index, site] = q
            residual = residual_in[index][site] - alpha * q
            residual_ref[index, site] = residual
            block.append(residual.astype(jnp.bfloat16))
            if index == 0:
                own.append(residual)
        blocks.append(block)
    mapped = products(rows, links_ref, table_ref, plane_ref, blocks)
    for site in sites:
        mapped_ref[site] = mapped[site]
    pairs = [
        ([older[0, site] for site in sites], mapped) for older in list(basis) + [new_ref]
    ]
    inner_rows(pairs + [(mapped, mapped), (mapped, own)], dots_ref)


def last_kernel(rows, last, *refs):
    refs = list(refs)
    gathered = refs[: last + 1]
    mapped_ref = refs[last + 1]
    residuals = refs[last + 2 : 2 * last + 3]
    basis = refs[2 * last + 3 : 3 * last + 3]
    solution_ref, residual_ref = refs[3 * last + 3 :]
    rhs = mapped_ref.shape[1]
    steps = [weights(ref[...], index, rhs) for index, ref in enumerate(gathered)]
    coefficients, inverse, alpha = steps[last]
    for site in range(rows["sites"]):
        q = mapped_ref[site]
        for weight, older in zip(coefficients, basis):
            q = q - weight * older[0, site]
        q = q * inverse
        current = [residuals[0][site]] + [ref[0, site] for ref in residuals[1:]]
        residual_ref[:, site, :] = current[last] - alpha * q
        found = []
        solution = None
        for index in range(last + 1):
            p = current[index].astype(jnp.bfloat16).astype(jnp.float32)
            for weight, older in zip(steps[index][0], found):
                p = p - weight * older
            p = p * steps[index][1]
            found.append(p)
            term = steps[index][2] * p
            solution = term if solution is None else solution + term
        solution_ref[:, site, :] = solution


def call(body, outs, operands, flops, table=None, scratch=()):
    vmem = pl.BlockSpec(memory_space=pltpu.VMEM)
    specs = [vmem] * len(operands)
    if table is not None:
        specs = [pl.BlockSpec(memory_space=pltpu.SMEM)] + specs
        operands = [table] + list(operands)
    size = sum(int(np.prod(v.shape)) * v.dtype.itemsize for v in list(outs) + list(operands))
    return pl.pallas_call(
        body,
        out_shape=tuple(outs),
        in_specs=specs,
        out_specs=tuple([vmem] * len(outs)),
        scratch_shapes=list(scratch),
        compiler_params=pltpu.CompilerParams(vmem_limit_bytes=16 * 1024 * 1024),
        cost_estimate=pl.CostEstimate(flops=flops, bytes_accessed=size, transcendentals=0),
    )(*operands)


def gather_all(dots):
    return lax.all_to_all(dots, AXES, 0, 0, tiled=True)


def local(coarse_links, right_sides):
    f32 = jnp.float32
    rhs, _, _, site_count, width = right_sides.shape
    group = lax.axis_size("grp")
    devices = group * lax.axis_size("ta") * lax.axis_size("gz")
    own = jnp.swapaxes(right_sides[:, 0, 0], 0, 1)
    table = site_table()
    rows = {"plane": group, "sites": site_count, "blocks": group + 4, "neighbours": None}
    dynamic = None
    scratch = [pltpu.VMEM((group * site_count, rhs, width), jnp.bfloat16)]
    if site_count % LX == 0:
        rows["neighbours"] = table[:site_count].tolist()
    else:
        offset = lax.axis_index("grp") * site_count
        places = lax.dynamic_slice_in_dim(jnp.asarray(table), offset, site_count, 0)
        dynamic = (places - offset + table.shape[0]) % table.shape[0]
    residual = [own] + exchange(own)
    links = arranged_links(coarse_links, site_count)
    flops = 2 * int(np.prod(links.shape)) * rhs
    slab = (rows["blocks"], site_count, rhs, width)

    def entry(body, *settings):
        settings = settings if dynamic is not None else settings + (None,)
        return functools.partial(body, *settings)

    def dots_shape(count):
        return jax.ShapeDtypeStruct((devices, -(-count * rhs // LANES) * LANES), f32)

    field = jax.ShapeDtypeStruct((site_count, rhs, width), f32)
    mapped, dots = call(
        entry(first_kernel, rows),
        [field, dots_shape(2)],
        [links] + residual,
        flops,
        dynamic,
        scratch,
    )
    gathered = []
    own_residuals = [own]
    basis = []
    for previous in range(ITERS - 1):
        gathered.append(gather_all(dots))
        halo = exchange(mapped)
        full = jax.ShapeDtypeStruct(slab, f32)
        mapped, dots, stacked, new = call(
            entry(next_kernel, rows, previous),
            [field, dots_shape(previous + 3), full, full],
            [links, gathered[-1], mapped] + halo + residual + basis,
            flops,
            dynamic,
            scratch,
        )
        residual = [stacked]
        own_residuals.append(stacked)
        basis.append(new)
    gathered.append(gather_all(dots))
    out = jax.ShapeDtypeStruct((rhs, site_count, width), f32)
    found, left = call(
        functools.partial(last_kernel, rows, ITERS - 1),
        [out, out],
        gathered + [mapped] + own_residuals + basis,
        flops // 100,
    )
    return (found.reshape(right_sides.shape), left.reshape(right_sides.shape))


def solution(mesh):
    placed = (P("ta", "gz", None, None, None, None), P(None, "ta", "gz", "grp", None))
    return jax.shard_map(
        local,
        mesh=mesh,
        in_specs=placed,
        out_specs=(P(None, "ta", "gz", "grp", None), P(None, "ta", "gz", "grp", None)),
        check_vma=False,
    )
```

```python
import functools

import jax
import jax.numpy as jnp
import numpy as np
from jax import lax
from jax.experimental import pallas as pl
from jax.experimental.pallas import tpu as pltpu
from jax.sharding import PartitionSpec as P


LX = 4
LY = 4
ITERS = 4
AXES = ("grp", "ta", "gz")
LANES = 128
GRANT = 16 * 1024 * 1024
CHIP_ROOM = 9400 * 1024


def site_table():
    site_ids = np.arange(LX * LY)
    column = site_ids % LX
    row_of = site_ids // LX
    forward_x = row_of * LX + (column + 1) % LX
    backward_x = row_of * LX + (column - 1) % LX
    forward_y = (row_of + 1) % LY * LX + column
    backward_y = (row_of - 1) % LY * LX + column
    return np.stack([forward_x, backward_x, forward_y, backward_y], axis=1).astype(np.int32)


def pairings(count):
    if count % 2 == 0:
        first = [(i, i ^ 1) for i in range(count)]
        second = [(i, (i + 1) % count if i % 2 else (i - 1) % count) for i in range(count)]
        return first, second, True
    up = [((i + 1) % count, i) for i in range(count)]
    return up, [(target, source) for source, target in up], False


def exchange(block):
    count = lax.axis_size("grp")
    blocks = []
    for shift in range(1, count):
        pairs = [((i + shift) % count, i) for i in range(count)]
        blocks.append(lax.ppermute(block, "grp", pairs))
    for axis in ("ta", "gz"):
        first, second, _ = pairings(lax.axis_size(axis))
        for pairs in (first, second):
            blocks.append(lax.ppermute(block, axis, pairs))
    return blocks


def link_places():
    order = [0, 1, 2, 3, 4]
    for axis, base in (("ta", 7), ("gz", 5)):
        odd = lax.axis_index(axis) % 2 if pairings(lax.axis_size(axis))[2] else 0
        order += [base + odd, base + 1 - odd]
    return order


def arrange_kernel(held, links_ref, *refs):
    *outs, raw, turned, arrived, left = refs
    count = raw.shape[0]
    offset = lax.axis_index("grp") * count
    order = link_places()
    width = raw.shape[2]
    incoming = [
        pltpu.make_async_copy(links_ref.at[offset + site], raw.at[site], arrived.at[site])
        for site in range(count)
    ]
    for copy in incoming:
        copy.start()
    outgoing = []
    for site in reversed(range(count)):
        incoming[site].wait()
        target = outs[0].at[site] if site < held else turned.at[site - held]
        for place, hop in enumerate(order):
            target[place * width : (place + 1) * width, :] = raw[site, hop].T
        if site >= held:
            place = site - held
            copy = pltpu.make_async_copy(target, outs[-1].at[place], left.at[place])
            copy.start()
            outgoing.append(copy)
    for copy in outgoing:
        copy.wait()


def arranged_links(links, count, held):
    _, hops, width, depth = links.shape
    site = (hops * depth, width)
    rest = count - held
    vmem, hbm = pl.BlockSpec(memory_space=pltpu.VMEM), pl.BlockSpec(memory_space=pltpu.HBM)
    outs, specs = [], []
    if held:
        outs.append(jax.ShapeDtypeStruct((held,) + site, links.dtype))
        specs.append(vmem)
    if rest:
        outs.append(pltpu.HBM((rest,) + site, links.dtype))
        specs.append(hbm)
    size = 2 * count * int(np.prod(site)) * links.dtype.itemsize
    return pl.pallas_call(
        functools.partial(arrange_kernel, held),
        out_shape=tuple(outs),
        in_specs=[hbm],
        out_specs=tuple(specs),
        scratch_shapes=[
            pltpu.VMEM((count,) + links.shape[1:], links.dtype),
            pltpu.VMEM((max(rest, 1),) + site, links.dtype),
            pltpu.SemaphoreType.DMA((count,)),
            pltpu.SemaphoreType.DMA((max(rest, 1),)),
        ],
        compiler_params=pltpu.CompilerParams(vmem_limit_bytes=GRANT),
        cost_estimate=pl.CostEstimate(flops=0, bytes_accessed=size, transcendentals=0),
    )(pltpu.with_memory_space_constraint(links, pltpu.HBM))


class Field:
    def __init__(self, ref, given=None):
        self.ref = ref
        self.given = given

    def place(self, site):
        if self.given is None:
            return site
        return pl.ds(site, self.ref.shape[0] // self.given, stride=self.given)

    def __getitem__(self, site):
        return self.ref[self.place(site)]

    def __setitem__(self, site, value):
        self.ref[self.place(site)] = value


def columns(gathered, count, rhs):
    total = jnp.sum(gathered, axis=0, keepdims=True)
    spread = jnp.broadcast_to(total, (rhs, total.shape[1]))
    lane = lax.broadcasted_iota(jnp.int32, spread.shape, 1)
    row = lax.broadcasted_iota(jnp.int32, spread.shape, 0)
    return [
        jnp.sum(jnp.where(lane == row + index * rhs, spread, 0.0), axis=1, keepdims=True)
        for index in range(count)
    ]


def weights(gathered, previous, rhs):
    values = columns(gathered, previous + 2, rhs)
    coefficients = values[:previous]
    squared, projected = values[previous], values[previous + 1]
    for value in coefficients:
        squared = squared - value * value
    inverse = 1.0 / jnp.sqrt(squared)
    return coefficients, inverse, projected * inverse


class Links:
    def __init__(self, rows, refs, landing, arrived):
        self.held = rows["held"]
        self.chip = refs[0] if self.held else None
        self.landing = landing
        self.copies = []
        for place in range(rows["sites"] - self.held):
            copy = pltpu.make_async_copy(refs[-1].at[place], landing.at[place], arrived.at[place])
            copy.start()
            self.copies.append(copy)

    def __getitem__(self, site):
        if site < self.held:
            return self.chip[site]
        self.copies[site - self.held].wait()
        return self.landing[site - self.held]


def products(rows, links, table_ref, plane_ref, blocks):
    plane = [value for block in blocks[: rows["plane"]] for value in block]
    neighbours = rows["neighbours"]
    if neighbours is None:
        for index, value in enumerate(plane):
            plane_ref[index] = value
    result = []
    for site in range(rows["sites"]):
        parts = [blocks[0][site]]
        if neighbours is None:
            parts += [plane_ref[table_ref[site, hop]] for hop in range(4)]
        else:
            parts += [plane[index] for index in neighbours[site]]
        parts += [block[site] for block in blocks[rows["plane"] :]]
        result.append(
            jnp.dot(
                jnp.concatenate(parts, axis=1), links[site], preferred_element_type=jnp.float32
            )
        )
    return result


def inner_rows(pairs, out_ref):
    stacked = []
    for left, right in pairs:
        total = left[0] * right[0]
        for a, b in zip(left[1:], right[1:]):
            total = total + a * b
        stacked.append(total)
    height = sum(value.shape[0] for value in stacked)
    if out_ref.shape[1] > height:
        stacked.append(jnp.zeros((out_ref.shape[1] - height, stacked[0].shape[1]), jnp.float32))
    table = jnp.concatenate(stacked, axis=0)
    ones = jnp.ones((out_ref.shape[0], table.shape[1]), jnp.float32)
    out_ref[...] = lax.dot_general(
        ones,
        table,
        (((1,), (1,)), ((), ())),
        precision=lax.Precision.HIGHEST,
        preferred_element_type=jnp.float32,
    )


def first_kernel(rows, *refs):
    refs = list(refs)
    *refs, plane_ref, landing, arrived = refs
    table_ref, refs = (None, refs) if rows["neighbours"] else (refs[0], refs[1:])
    links = Links(rows, refs[: rows["parts"]], landing, arrived)
    *residual_refs, mapped_ref, dots_ref = refs[rows["parts"] :]
    sites = range(rows["sites"])
    residual_refs = [Field(ref, rows["sites"]) for ref in residual_refs]
    blocks = [[ref[site].astype(jnp.bfloat16) for site in sites] for ref in residual_refs]
    mapped = products(rows, links, table_ref, plane_ref, blocks)
    own = [residual_refs[0][site] for site in sites]
    for site in sites:
        mapped_ref[site] = mapped[site]
    inner_rows([(mapped, mapped), (mapped, own)], dots_ref)


def next_kernel(rows, previous, *refs):
    refs = list(refs)
    *refs, plane_ref, landing, arrived = refs
    table_ref, refs = (None, refs) if rows["neighbours"] else (refs[0], refs[1:])
    links = Links(rows, refs[: rows["parts"]], landing, arrived)
    gathered_ref, *refs = refs[rows["parts"] :]
    count = rows["blocks"]
    sites = range(rows["sites"])

    def field(stacked):
        own = refs.pop(0)
        if stacked:
            halo = refs.pop(0)
            return [own] + [halo.at[index] for index in range(count - 1)]
        return [own] + [refs.pop(0) for _ in range(count - 1)]

    mapped_in = field(False)
    residual_in = field(previous > 0)
    if previous == 0:
        residual_in = [Field(ref, rows["sites"]) for ref in residual_in]
    basis = [field(True) for _ in range(previous)]
    mapped_ref, dots_ref = refs.pop(0), refs.pop(0)
    keep_halo = previous < ITERS - 2
    outs = [field(True) if keep_halo else [refs.pop(0)] for _ in range(2)]
    rhs = mapped_in[0].shape[1]
    coefficients, inverse, alpha = weights(gathered_ref[...], previous, rhs)
    blocks = []
    own = []
    for index in range(count):
        block = []
        for site in sites:
            q = mapped_in[index][site]
            for weight, older in zip(coefficients, basis):
                q = q - weight * older[index][site]
            q = q * inverse
            residual = residual_in[index][site] - alpha * q
            if keep_halo or index == 0:
                outs[0][index][site] = residual
                outs[1][index][site] = q
            block.append(residual.astype(jnp.bfloat16))
            if index == 0:
                own.append(residual)
        blocks.append(block)
    mapped = products(rows, links, table_ref, plane_ref, blocks)
    for site in sites:
        mapped_ref[site] = mapped[site]
    pairs = [
        ([older[site] for site in sites], mapped)
        for older in [field_refs[0] for field_refs in basis] + [outs[1][0]]
    ]
    inner_rows(pairs + [(mapped, mapped), (mapped, own)], dots_ref)


def last_kernel(rows, last, *refs):
    gathered, refs = refs[: last + 1], refs[last + 1 :]
    mapped_ref, refs = refs[0], refs[1:]
    residuals, basis, (solution_ref, residual_ref) = (
        refs[: last + 1],
        refs[last + 1 : 2 * last + 1],
        refs[2 * last + 1 :],
    )
    residuals = [Field(residuals[0], rows["sites"])] + list(residuals[1:])
    solution_ref, residual_ref = (Field(ref, rows["sites"]) for ref in (solution_ref, residual_ref))
    rhs = mapped_ref.shape[1]
    steps = [weights(ref[...], index, rhs) for index, ref in enumerate(gathered)]
    coefficients, inverse, alpha = steps[last]
    for site in range(rows["sites"]):
        q = mapped_ref[site]
        for weight, older in zip(coefficients, basis):
            q = q - weight * older[site]
        q = q * inverse
        residual_ref[site] = residuals[last][site] - alpha * q
        found = []
        solution = None
        for index in range(last + 1):
            p = residuals[index][site].astype(jnp.bfloat16).astype(jnp.float32)
            for weight, older in zip(steps[index][0], found):
                p = p - weight * older
            p = p * steps[index][1]
            found.append(p)
            term = steps[index][2] * p
            solution = term if solution is None else solution + term
        solution_ref[site] = solution


def call(body, outs, operands, flops, links=(), table=None, scratch=()):
    vmem = pl.BlockSpec(memory_space=pltpu.VMEM)
    specs = [vmem] * len(operands)
    lead, lead_specs = [], []
    if table is not None:
        lead.append(table)
        lead_specs.append(pl.BlockSpec(memory_space=pltpu.SMEM))
    for value, on_chip in links:
        lead.append(value if on_chip else pltpu.with_memory_space_constraint(value, pltpu.HBM))
        lead_specs.append(vmem if on_chip else pl.BlockSpec(memory_space=pltpu.HBM))
    size = sum(int(np.prod(v.shape)) * v.dtype.itemsize for v in list(outs) + list(operands))
    return pl.pallas_call(
        body,
        out_shape=tuple(outs),
        in_specs=lead_specs + specs,
        out_specs=tuple([vmem] * len(outs)),
        scratch_shapes=list(scratch),
        compiler_params=pltpu.CompilerParams(vmem_limit_bytes=GRANT),
        cost_estimate=pl.CostEstimate(flops=flops, bytes_accessed=size, transcendentals=0),
    )(*lead, *operands)


def gather_all(dots):
    return lax.all_to_all(dots, AXES, 0, 0, tiled=True)


def local(coarse_links, right_sides):
    f32 = jnp.float32
    rhs, _, _, site_count, width = right_sides.shape
    hops = coarse_links.shape[3]
    group = lax.axis_size("grp")
    devices = group * lax.axis_size("ta") * lax.axis_size("gz")
    blocks = group + 4
    own = right_sides.reshape(rhs * site_count, width)
    table = site_table()
    field_bytes = site_count * rhs * width * 4
    site_bytes = hops * width * width * coarse_links.dtype.itemsize
    room = CHIP_ROOM - (ITERS * blocks + ITERS) * field_bytes
    held = max(0, min(site_count, room // site_bytes))
    rows = {
        "plane": group,
        "sites": site_count,
        "blocks": blocks,
        "neighbours": None,
        "held": held,
        "parts": (held > 0) + (held < site_count),
    }
    dynamic = None
    if site_count % LX == 0:
        rows["neighbours"] = table[:site_count].tolist()
    else:
        offset = lax.axis_index("grp") * site_count
        places = lax.dynamic_slice_in_dim(jnp.asarray(table), offset, site_count, 0)
        dynamic = (places - offset + table.shape[0]) % table.shape[0]
    halo = exchange(own)
    parts = arranged_links(coarse_links[0, 0], site_count, held)
    links = [(value, held > 0 and index == 0) for index, value in enumerate(parts)]
    flops = 2 * site_count * hops * width * width * rhs
    rest = max(site_count - held, 1)
    scratch = [
        pltpu.VMEM((group * site_count, rhs, width), jnp.bfloat16),
        pltpu.VMEM((rest, hops * width, width), coarse_links.dtype),
        pltpu.SemaphoreType.DMA((rest,)),
    ]
    one = jax.ShapeDtypeStruct((site_count, rhs, width), f32)
    several = jax.ShapeDtypeStruct((blocks - 1, site_count, rhs, width), f32)

    def dots_shape(count):
        return jax.ShapeDtypeStruct((devices, -(-count * rhs // LANES) * LANES), f32)

    mapped, dots = call(
        functools.partial(first_kernel, rows),
        [one, dots_shape(2)],
        [own] + halo,
        flops,
        links,
        dynamic,
        scratch,
    )
    gathered = []
    residuals = [[own] + halo]
    basis = []
    for previous in range(ITERS - 1):
        gathered.append(gather_all(dots))
        halo = exchange(mapped)
        kept = [one, several] if previous < ITERS - 2 else [one]
        mapped, dots, *rest = call(
            functools.partial(next_kernel, rows, previous),
            [one, dots_shape(previous + 3)] + kept + kept,
            [gathered[-1], mapped] + halo + residuals[-1] + [ref for pair in basis for ref in pair],
            flops,
            links,
            dynamic,
            scratch,
        )
        residuals.append(rest[: len(kept)])
        basis.append(rest[len(kept) :])
    gathered.append(gather_all(dots))
    out = jax.ShapeDtypeStruct(own.shape, f32)
    found, left = call(
        functools.partial(last_kernel, rows, ITERS - 1),
        [out, out],
        gathered + [mapped] + [pair[0] for pair in residuals] + [pair[0] for pair in basis],
        flops // 100,
    )
    return (found.reshape(right_sides.shape), left.reshape(right_sides.shape))


def solution(mesh):
    placed = (P("ta", "gz", None, None, None, None), P(None, "ta", "gz", "grp", None))
    return jax.shard_map(
        local,
        mesh=mesh,
        in_specs=placed,
        out_specs=(P(None, "ta", "gz", "grp", None), P(None, "ta", "gz", "grp", None)),
        check_vma=False,
    )
```
